256 devices in a mesh: seq: 2 (over core), expert: 128 (over y, x, z).
Axes of the slice: x: 4, y: 4, z: 8, core: 2. Of those that a mesh axis runs over, the one named last changes fastest.
Arguments:
- tokens: bfloat16 [32768, 4096], P(('seq', 'expert')), may hold values from -6 to 6
- routes: int32 [32768, 2], P(('seq', 'expert')), may hold values from 0 to 127, all different within a row; in each aligned block of 128 rows (0 to 127, 128 to 255, ...) at most 3 rows name the same one
- route_probs: float32 [32768, 2], P(('seq', 'expert')), may hold values from 0.25 to 1
- gate_weight: bfloat16 [128, 4096, 768], P('expert', None, 'seq'), may hold values from -0.09375 to 0.09375
- up_weight: bfloat16 [128, 4096, 768], P('expert', None, 'seq'), may hold values from -0.09375 to 0.09375
- down_weight: bfloat16 [128, 768, 4096], P('expert', 'seq'), may hold values from -0.21875 to 0.21875
- grad_out: bfloat16 [32768, 4096], P(('seq', 'expert')), may hold values from -3 to 3
Outputs:
- grad_tokens: bfloat16 [32768, 4096], P(('seq', 'expert'))
- grad_probs: bfloat16 [32768, 2], P(('seq', 'expert'))
The draws below stay inside these ranges and needn't reach their ends.
Inputs may be any that keep to these rules, and one draw needn't show every extreme that they name: `routes`: each token names 2 different experts. Among the tokens of one device no expert is named by more than 3 tokens, and in every draw some device names some expert exactly 3 times.
All inputs are finite; a program needn't handle non-finite values.
Results may differ from the reference program's by a relative error of at most 0.01.
Values may be sent and summed in bfloat16 or wider, within the bound.
No kernel may reach another device: no remote copies, remote signals or barrier semaphores. Data moves between devices by JAX's collectives and lax.ppermute only.
A program may use at most 128 MiB of HBM per device.

```python
import math
import jax
import jax.numpy as jnp
import numpy as np
from jax import lax

D = 4096
H = 768
TOPK = 2
TOK_DEV = 128
EXPERTS = 128
CAP = 3
TOKENS = 32768
N_SEQ = 2
N_EXPERT = 128


def block_levels(stream_key, shape, split, least, top_value):
    loudness = 1.0
    for position, blocks in split:
        draws = jax.random.uniform(jax.random.fold_in(jax.random.fold_in(stream_key, 6), position), (blocks,), jnp.float32, least / len(split), top_value / len(split))
        loudness = loudness * jnp.repeat(jnp.exp(draws), shape[position] // blocks).reshape((-1,) + (1,) * (len(shape) - 1 - position))
    return loudness


def shared_out(stream_key, own, number, rows, number_of, top, reach, slope):
    sequence = jax.random.permutation(stream_key, number_of)
    packed, usual = load_shares(number_of, rows * top, reach, slope, True), load_shares(number_of, rows * top, reach, slope, False)
    places = jnp.arange(number_of)

    def named(lengths, rotation):
        used = int((lengths > 0).sum())
        fixed = max(1, used // 4)
        moved = fixed + (places - fixed + rotation * (used - fixed)) % max(1, number_of - fixed)
        return jnp.zeros((number_of,), jnp.int32).at[sequence[jnp.where(places < fixed, places, moved)]].set(jnp.asarray(lengths, jnp.int32))

    lengths = jnp.where(number % 4 == 0, named(packed, number // 4), named(usual, number - number // 4 - 1))
    mixed = jax.random.permutation(jax.random.fold_in(own, 3), number_of)
    donor, sink = mixed[0:number_of // 2 * 2:2], mixed[1:number_of // 2 * 2:2]
    margin = jnp.minimum(lengths[donor] - 1, reach - lengths[sink]) // 2
    margin = jnp.where((donor == sequence[0]) | (sink == sequence[0]) | (lengths[sink] == 0), 0, jnp.maximum(margin, 0))
    moved = jax.random.randint(jax.random.fold_in(own, 4), (number_of // 2,), 0, 1 << 20) % (margin + 1)
    lengths = lengths.at[donor].add(-moved).at[sink].add(moved)
    members = jnp.searchsorted(jnp.cumsum(lengths), jnp.arange(rows * top), side="right").astype(jnp.int32)
    grid = members.reshape(top, rows).T
    grid = grid[jax.random.permutation(jax.random.fold_in(own, 1), rows)]
    rotation = jax.random.randint(jax.random.fold_in(own, 2), (rows, 1), 0, top)
    return jnp.take_along_axis(grid, (jnp.arange(top)[None, :] + rotation) % top, axis=1)


def load_shares(amount, total, limit, slope, full):
    weights = [(1 << 20) // math.isqrt(standing ** slope) + 1 for standing in range(1, amount + 1)]
    largest = limit if full else min(limit, max(-(-total // amount), total * weights[0] // sum(weights)))
    least = 1 if total - largest >= amount - 1 else 0
    given, surplus = [largest] + [least] * (amount - 1), total - largest - least * (amount - 1)
    while surplus > 0:
        free = [i for i in range(1, amount) if given[i] < largest] or [i for i in range(1, amount) if given[i] < limit]
        mass, remaining = sum([weights[i] for i in free]), surplus
        for i in free:
            more = min(limit - given[i], max(1, remaining * weights[i] // mass), surplus)
            given[i] = given[i] + more
            surplus = surplus - more
    return np.array(given)


def gaussian(rng, extent, scale, bound, split=(), kind=jnp.bfloat16):
    entries = scale * jax.random.normal(rng, extent, jnp.float32)
    if split:
        entries = entries * block_levels(rng, extent, split, -0.22, 0.18)
    return jnp.clip(entries, -bound, bound).astype(kind)


def setup_inputs(seed: int = 0) -> dict:
    key_of = jax.random.split(jax.random.key(seed), 8)
    tokens = gaussian(key_of[0], (TOKENS, D), 1.0, 6.0, ((0, 256),))
    routes_keys = jax.random.split(jax.random.fold_in(key_of[1], 1), TOKENS // TOK_DEV)
    routes_turns = jax.random.permutation(jax.random.fold_in(key_of[1], 3), TOKENS // TOK_DEV)
    routes = jax.vmap(lambda own, number: shared_out(jax.random.fold_in(key_of[1], 2), own, number, TOK_DEV, EXPERTS, TOPK, CAP, 1))(routes_keys, routes_turns).reshape((TOKENS, TOPK))
    route_probs = jnp.clip(0.25 + 0.75 * jax.random.uniform(key_of[2], (TOKENS, TOPK), jnp.float32) ** block_levels(key_of[2], (TOKENS, TOPK), ((0, 256),), -0.2, 0.2), 0.25, 1.0)
    gate_weight = gaussian(key_of[3], (EXPERTS, D, H), D ** -0.5, 0.09375, ((0, 128), (2, 2)))
    up_weight = gaussian(key_of[4], (EXPERTS, D, H), D ** -0.5, 0.09375, ((0, 128), (2, 2)))
    down_weight = gaussian(key_of[5], (EXPERTS, H, D), H ** -0.5, 0.21875, ((0, 128), (1, 2)))
    grad_out = gaussian(key_of[6], (TOKENS, D), 0.5, 3.0, ((0, 256),))
    return dict(tokens=tokens, routes=routes, route_probs=route_probs, gate_weight=gate_weight, up_weight=up_weight, down_weight=down_weight, grad_out=grad_out)


def expert_terms(rows_in, rows_grad, gate_w, up_w, down_w):
    contract = (((1,), (1,)), ((), ()))
    gating = jnp.dot(rows_in, gate_w, preferred_element_type=jnp.float32)
    lifted = jnp.dot(rows_in, up_w, preferred_element_type=jnp.float32)
    sigmoid = jax.nn.sigmoid(gating)
    active = gating * sigmoid
    hidden = (active * lifted).astype(jnp.bfloat16)
    grad_hidden = lax.dot_general(rows_grad, down_w, contract, preferred_element_type=jnp.float32)
    grad_prob = jnp.sum(hidden.astype(jnp.float32) * grad_hidden, axis=1)
    slope_term = sigmoid * (1.0 + gating * (1.0 - sigmoid))
    grad_gate = (grad_hidden * lifted * slope_term).astype(jnp.bfloat16)
    grad_up = (grad_hidden * active).astype(jnp.bfloat16)
    grad_rows = lax.dot_general(grad_gate, gate_w, contract, preferred_element_type=jnp.float32)
    grad_rows = grad_rows + lax.dot_general(grad_up, up_w, contract, preferred_element_type=jnp.float32)
    return grad_rows, grad_prob


def reference(tokens, routes, route_probs, gate_weight, up_weight, down_weight, grad_out):
    total = TOKENS * TOPK
    chosen = routes.reshape(-1).astype(jnp.int32)
    ordering = jnp.argsort(chosen, stable=True).astype(jnp.int32)
    counts = jnp.zeros((EXPERTS,), jnp.int32).at[chosen].add(1)
    offsets = (jnp.cumsum(counts) - counts).astype(jnp.int32)
    row_limit = CAP * N_EXPERT * N_SEQ
    flat_probs = route_probs.reshape(-1)

    def per_expert(totals, expert):
        grad_acc, prob_acc = totals
        lanes = jnp.arange(row_limit, dtype=jnp.int32)
        flat_index = jnp.clip(offsets[expert] + lanes, 0, total - 1).astype(jnp.int32)
        is_live = lanes < counts[expert]
        assigned = ordering[flat_index]
        source = (assigned // TOPK).astype(jnp.int32)
        grad_rows, grad_prob = expert_terms(tokens[source], grad_out[source], gate_weight[expert], up_weight[expert], down_weight[expert])
        grad_rows = lax.optimization_barrier(grad_rows.astype(jnp.bfloat16))
        grad_prob = lax.optimization_barrier(grad_prob.astype(jnp.bfloat16))
        weighting = jnp.where(is_live, flat_probs[assigned], 0.0).astype(jnp.float32)
        grad_acc = grad_acc.at[source].add(weighting[:, None] * grad_rows.astype(jnp.float32))
        prob_acc = prob_acc.at[assigned].add(jnp.where(is_live, grad_prob.astype(jnp.float32), 0.0))
        return (grad_acc, prob_acc), None

    start = (jnp.zeros((TOKENS, D), jnp.float32), jnp.zeros((total,), jnp.float32))
    (grad_acc, prob_acc), _ = lax.scan(per_expert, start, jnp.arange(EXPERTS, dtype=jnp.int32))
    return grad_acc.astype(jnp.bfloat16), prob_acc.reshape(TOKENS, TOPK).astype(jnp.bfloat16)
```

```python
import functools

import jax
import jax.numpy as jnp
from jax import lax
from jax.experimental import pallas as pl
from jax.experimental.pallas import tpu as pltpu
from jax.sharding import PartitionSpec as P

LANES = 128
CHUNK = 8
VMEM_LIMIT = 56 * 1024 * 1024


def params():
    return pltpu.CompilerParams(vmem_limit_bytes=VMEM_LIMIT)


def to_blocks(x_ref, wide):
    rows, width = x_ref.shape
    parts = width // LANES
    for c in range(parts):
        wide[pl.ds(c, rows, stride=parts), :] = x_ref[:, c * LANES : (c + 1) * LANES].astype(
            jnp.float32
        )


def route_kernel(capacity, routes_ref, x_ref, slots_ref, out_ref, counts, wide):
    top, tok_count = routes_ref.shape
    parts = x_ref.shape[1] // LANES
    out_ref[...] = jnp.zeros_like(out_ref)

    def clear(e, _):
        counts[e] = 0
        return 0

    lax.fori_loop(0, counts.shape[0], clear, 0)
    to_blocks(x_ref, wide)

    def place(t, _):
        row = wide[pl.ds(pl.multiple_of(t * parts, parts), parts), :].astype(jnp.bfloat16)
        for k in range(top):
            e = routes_ref[k, t]
            position = counts[e]
            counts[e] = position + 1
            slot = e * capacity + position
            slots_ref[k, t] = slot
            out_ref[slot] = row
        return 0

    lax.fori_loop(0, tok_count, place, 0)


def route_and_place(routes, x, expert_count, capacity):
    tok_count, width = x.shape
    top = routes.shape[0]
    parts = width // LANES
    return pl.pallas_call(
        functools.partial(route_kernel, capacity),
        out_shape=(
            jax.ShapeDtypeStruct((top, tok_count), jnp.int32),
            jax.ShapeDtypeStruct((expert_count * capacity, parts, LANES), jnp.bfloat16),
        ),
        in_specs=[
            pl.BlockSpec(memory_space=pltpu.SMEM),
            pl.BlockSpec(memory_space=pltpu.VMEM),
        ],
        out_specs=(
            pl.BlockSpec(memory_space=pltpu.SMEM),
            pl.BlockSpec(memory_space=pltpu.VMEM),
        ),
        scratch_shapes=[
            pltpu.SMEM((expert_count,), jnp.int32),
            pltpu.VMEM((tok_count * parts, LANES), jnp.float32),
        ],
        compiler_params=params(),
        name="route_and_place",
    )(routes, x)


def place_kernel(slots_ref, x_ref, out_ref, wide):
    top, tok_count = slots_ref.shape
    parts = x_ref.shape[1] // LANES
    out_ref[...] = jnp.zeros_like(out_ref)
    to_blocks(x_ref, wide)

    def place(t, _):
        row = wide[pl.ds(pl.multiple_of(t * parts, parts), parts), :].astype(jnp.bfloat16)
        for k in range(top):
            out_ref[slots_ref[k, t]] = row
        return 0

    lax.fori_loop(0, tok_count, place, 0)


def place_rows(slots, x, slot_count):
    tok_count, width = x.shape
    parts = width // LANES
    return pl.pallas_call(
        place_kernel,
        out_shape=jax.ShapeDtypeStruct((slot_count, parts, LANES), jnp.bfloat16),
        in_specs=[
            pl.BlockSpec(memory_space=pltpu.SMEM),
            pl.BlockSpec(memory_space=pltpu.VMEM),
        ],
        out_specs=pl.BlockSpec(memory_space=pltpu.VMEM),
        scratch_shapes=[pltpu.VMEM((tok_count * parts, LANES), jnp.float32)],
        compiler_params=params(),
        name="place_rows",
    )(slots, x)


def load_rows(x_ref, wide, rows_scr):
    rows = x_ref.shape[0]
    wide[...] = x_ref[...].astype(jnp.float32).reshape(rows * CHUNK, LANES)
    for c in range(CHUNK):
        rows_scr[:, c * LANES : (c + 1) * LANES] = wide[pl.ds(c, rows, stride=CHUNK), :].astype(
            jnp.bfloat16
        )


def forward_kernel(x_ref, g0, g1, u0, u1, hidden_ref, slope_ref, active_ref, wide, rows_scr, acc_g, acc_u):
    step = pl.program_id(0)

    @pl.when(step == 0)
    def _():
        acc_g[...] = jnp.zeros_like(acc_g)
        acc_u[...] = jnp.zeros_like(acc_u)

    load_rows(x_ref, wide, rows_scr)
    rows = rows_scr[...]
    gate = jnp.concatenate([g0[...], g1[...]], axis=1)
    acc_g[...] += jnp.dot(rows, gate, preferred_element_type=jnp.float32)
    up = jnp.concatenate([u0[...], u1[...]], axis=1)
    acc_u[...] += jnp.dot(rows, up, preferred_element_type=jnp.float32)

    @pl.when(step == pl.num_programs(0) - 1)
    def _():
        gating = acc_g[...]
        lifted = acc_u[...]
        sigmoid = jax.nn.sigmoid(gating)
        active = gating * sigmoid
        hidden_ref[...] = (active * lifted).astype(jnp.bfloat16)
        slope_ref[...] = lifted * (sigmoid * (1.0 + gating * (1.0 - sigmoid)))
        active_ref[...] = active


def forward_terms(x, g0, g1, u0, u1):
    rows, parts, _ = x.shape
    half = g0.shape[1]
    hid = 2 * half
    depth = CHUNK * LANES
    weight = pl.BlockSpec((depth, half), lambda i: (i, 0))
    whole = pl.BlockSpec((rows, hid), lambda i: (0, 0))
    return pl.pallas_call(
        forward_kernel,
        grid=(parts // CHUNK,),
        out_shape=(
            jax.ShapeDtypeStruct((rows, hid), jnp.bfloat16),
            jax.ShapeDtypeStruct((rows, hid), jnp.float32),
            jax.ShapeDtypeStruct((rows, hid), jnp.float32),
        ),
        in_specs=[pl.BlockSpec((rows, CHUNK, LANES), lambda i: (0, i, 0))] + [weight] * 4,
        out_specs=(whole, whole, whole),
        scratch_shapes=[
            pltpu.VMEM((rows * CHUNK, LANES), jnp.float32),
            pltpu.VMEM((rows, depth), jnp.bfloat16),
            pltpu.VMEM((rows, hid), jnp.float32),
            pltpu.VMEM((rows, hid), jnp.float32),
        ],
        compiler_params=params(),
        name="forward_terms",
    )(x, g0, g1, u0, u1)


def backward_kernel(
    half_steps, x_ref, d0, d1, g0, g1, u0, u1, hidden_ref, slope_ref, active_ref,
    out_ref, prob_ref, wide, rows_scr, acc, grad_gate, grad_up,
):
    step = pl.program_id(0)
    contract = (((1,), (1,)), ((), ()))

    @pl.when(step == 0)
    def _():
        acc[...] = jnp.zeros_like(acc)

    @pl.when(step < half_steps)
    def _():
        load_rows(x_ref, wide, rows_scr)
        down = jnp.concatenate([d0[...], d1[...]], axis=0)
        acc[...] += lax.dot_general(rows_scr[...], down, contract, preferred_element_type=jnp.float32)

    @pl.when(step == half_steps - 1)
    def _():
        grad_hidden = acc[...]
        prob = jnp.sum(hidden_ref[...].astype(jnp.float32) * grad_hidden, axis=1, keepdims=True)
        prob_ref[...] = jnp.broadcast_to(prob, prob_ref.shape).astype(jnp.bfloat16)
        grad_gate[...] = (grad_hidden * slope_ref[...]).astype(jnp.bfloat16)
        grad_up[...] = (grad_hidden * active_ref[...]).astype(jnp.bfloat16)

    @pl.when(step >= half_steps)
    def _():
        rows = x_ref.shape[0]
        gate = jnp.concatenate([g0[...], g1[...]], axis=1)
        total = lax.dot_general(grad_gate[...], gate, contract, preferred_element_type=jnp.float32)
        up = jnp.concatenate([u0[...], u1[...]], axis=1)
        total += lax.dot_general(grad_up[...], up, contract, preferred_element_type=jnp.float32)
        for c in range(CHUNK):
            wide[pl.ds(c, rows, stride=CHUNK), :] = total[:, c * LANES : (c + 1) * LANES]
        out_ref[...] = wide[...].reshape(rows, CHUNK, LANES).astype(jnp.bfloat16)


def backward_terms(x, d0, d1, g0, g1, u0, u1, hidden, slope, active):
    rows, parts, _ = x.shape
    half = g0.shape[1]
    hid = 2 * half
    depth = CHUNK * LANES
    steps = parts // CHUNK
    early = lambda i: jnp.minimum(i, steps - 1)
    late = lambda i: jnp.maximum(i - steps, 0)
    down = pl.BlockSpec((half, depth), lambda i: (0, early(i)))
    weight = pl.BlockSpec((depth, half), lambda i: (late(i), 0))
    whole = pl.BlockSpec((rows, hid), lambda i: (0, 0), pipeline_mode=pl.Buffered(1))
    return pl.pallas_call(
        functools.partial(backward_kernel, steps),
        grid=(2 * steps,),
        out_shape=(
            jax.ShapeDtypeStruct((rows, parts, LANES), jnp.bfloat16),
            jax.ShapeDtypeStruct((rows, LANES), jnp.bfloat16),
        ),
        in_specs=[pl.BlockSpec((rows, CHUNK, LANES), lambda i: (0, early(i), 0))]
        + [down] * 2
        + [weight] * 4
        + [whole] * 3,
        out_specs=(
            pl.BlockSpec((rows, CHUNK, LANES), lambda i: (0, late(i), 0)),
            pl.BlockSpec((rows, LANES), lambda i: (0, 0)),
        ),
        scratch_shapes=[
            pltpu.VMEM((rows * CHUNK, LANES), jnp.float32),
            pltpu.VMEM((rows, depth), jnp.bfloat16),
            pltpu.VMEM((rows, hid), jnp.float32),
            pltpu.VMEM((rows, hid), jnp.bfloat16),
            pltpu.VMEM((rows, hid), jnp.bfloat16),
        ],
        compiler_params=params(),
        name="backward_terms",
    )(x, d0, d1, g0, g1, u0, u1, hidden, slope, active)


def combine_kernel(slots_ref, probs_ref, back_ref, out_ref, wide):
    top, tok_count = slots_ref.shape
    parts = back_ref.shape[1]

    def gather(t, _):
        total = probs_ref[0, t] * back_ref[slots_ref[0, t]].astype(jnp.float32)
        for k in range(1, top):
            total += probs_ref[k, t] * back_ref[slots_ref[k, t]].astype(jnp.float32)
        wide[pl.ds(pl.multiple_of(t * parts, parts), parts), :] = total
        return 0

    lax.fori_loop(0, tok_count, gather, 0)
    for c in range(parts):
        out_ref[:, c * LANES : (c + 1) * LANES] = wide[pl.ds(c, tok_count, stride=parts), :].astype(
            jnp.bfloat16
        )


def combine_rows(slots, probs, back):
    top, tok_count = slots.shape
    parts = back.shape[1]
    return pl.pallas_call(
        combine_kernel,
        out_shape=jax.ShapeDtypeStruct((tok_count, parts * LANES), jnp.bfloat16),
        in_specs=[
            pl.BlockSpec(memory_space=pltpu.SMEM),
            pl.BlockSpec(memory_space=pltpu.SMEM),
            pl.BlockSpec(memory_space=pltpu.VMEM),
        ],
        out_specs=pl.BlockSpec(memory_space=pltpu.VMEM),
        scratch_shapes=[pltpu.VMEM((tok_count * parts, LANES), jnp.float32)],
        compiler_params=params(),
        name="combine_rows",
    )(slots, probs, back)


def exchange(blocks, expert_count):
    rows, parts, lanes = blocks.shape
    sent = blocks.reshape(expert_count, rows // expert_count * parts, lanes)
    got = lax.all_to_all(sent, "expert", split_axis=0, concat_axis=0, tiled=True)
    return got.reshape(rows, parts, lanes)


def on_device(tokens, routes, route_probs, gate_weight, up_weight, down_weight, grad_out):
    tok_count, model_width = tokens.shape
    top_count = routes.shape[1]
    expert_count = lax.axis_size("expert")
    capacity = 3 * tok_count * top_count // (2 * expert_count)
    swap = lambda w: lax.ppermute(w, "seq", [(0, 1), (1, 0)])
    gate, up, down = gate_weight[0], up_weight[0], down_weight[0]
    gate_far, up_far, down_far = swap(gate), swap(up), swap(down)

    slots, send_in = route_and_place(routes.T, tokens, expert_count, capacity)
    recv_in = exchange(send_in, expert_count)
    send_grad = place_rows(slots, grad_out, expert_count * capacity)
    recv_grad = exchange(send_grad, expert_count)
    hidden, slope, active = forward_terms(recv_in, gate, gate_far, up, up_far)
    out_rows, out_prob = backward_terms(
        recv_grad, down, down_far, gate, gate_far, up, up_far, hidden, slope, active
    )
    back_rows = exchange(out_rows, expert_count)
    grad_tokens = combine_rows(slots, route_probs.T, back_rows)

    all_prob = lax.all_gather(out_prob[:, 0], "expert", axis=0, tiled=False)
    mine = lax.dynamic_slice(
        all_prob, (0, lax.axis_index("expert") * capacity), (expert_count, capacity)
    )
    grad_probs = mine.reshape(-1)[slots.T]
    return (grad_tokens, grad_probs)


def solution(mesh):
    placed = (
        P(("seq", "expert"), None),
        P(("seq", "expert"), None),
        P(("seq", "expert"), None),
        P("expert", None, "seq"),
        P("expert", None, "seq"),
        P("expert", "seq", None),
        P(("seq", "expert"), None),
    )
    return jax.shard_map(
        on_device,
        mesh=mesh,
        in_specs=placed,
        out_specs=(P(("seq", "expert"), None), P(("seq", "expert"), None)),
        check_vma=False,
    )
```

```python
import functools

import jax
import jax.numpy as jnp
from jax import lax
from jax.experimental import pallas as pl
from jax.experimental.pallas import tpu as pltpu
from jax.sharding import PartitionSpec as P

LANES = 128
CHUNK = 8
VMEM_LIMIT = 58 * 1024 * 1024
VMEM = pl.BlockSpec(memory_space=pltpu.VMEM)
SMEM = pl.BlockSpec(memory_space=pltpu.SMEM)


def params():
    return pltpu.CompilerParams(vmem_limit_bytes=VMEM_LIMIT)


def on_chip(x):
    return pltpu.with_memory_space_constraint(x, pltpu.VMEM)


def to_blocks(x_ref, wide, blocks):
    rows, width = x_ref.shape
    parts = width // LANES
    for c in range(parts):
        wide[pl.ds(c, rows, stride=parts), :] = x_ref[:, c * LANES : (c + 1) * LANES].astype(
            jnp.float32
        )
    blocks[...] = wide[...].reshape(rows, parts, LANES).astype(jnp.bfloat16)


def place_all(routes_ref, position_ref, blocks, out_ref, capacity):
    top, tok_count = routes_ref.shape
    group = 8

    def place(g, _):
        first = g * group
        rows = [blocks[first + i] for i in range(group)]
        slots = [
            [routes_ref[k, first + i] * capacity + position_ref[k, first + i] for k in range(top)]
            for i in range(group)
        ]
        for row, targets in zip(rows, slots):
            for slot in targets:
                out_ref[slot] = row
        return 0

    lax.fori_loop(0, tok_count // group, place, 0)


def route_kernel(capacity, routes_ref, x_ref, position_ref, out_ref, counts, wide, blocks):
    top, tok_count = routes_ref.shape

    def clear(e, _):
        counts[e] = 0
        return 0

    lax.fori_loop(0, counts.shape[0], clear, 0, unroll=16)
    to_blocks(x_ref, wide, blocks)

    def rank(t, _):
        for k in range(top):
            e = routes_ref[k, t]
            position = counts[e]
            counts[e] = position + 1
            position_ref[k, t] = position
        return 0

    lax.fori_loop(0, tok_count, rank, 0, unroll=8)
    place_all(routes_ref, position_ref, blocks, out_ref, capacity)


def route_and_place(routes, x, expert_count, capacity):
    tok_count, width = x.shape
    parts = width // LANES
    return pl.pallas_call(
        functools.partial(route_kernel, capacity),
        out_shape=(
            jax.ShapeDtypeStruct(routes.shape, jnp.int32),
            jax.ShapeDtypeStruct((expert_count * capacity, parts, LANES), jnp.bfloat16),
        ),
        in_specs=[SMEM, VMEM],
        out_specs=(SMEM, VMEM),
        scratch_shapes=[
            pltpu.SMEM((expert_count,), jnp.int32),
            pltpu.VMEM((tok_count * parts, LANES), jnp.float32),
            pltpu.VMEM((tok_count, parts, LANES), jnp.bfloat16),
        ],
        compiler_params=params(),
        name="route_and_place",
    )(routes, x)


def place_kernel(capacity, routes_ref, position_ref, x_ref, out_ref, wide, blocks):
    to_blocks(x_ref, wide, blocks)
    place_all(routes_ref, position_ref, blocks, out_ref, capacity)


def place_rows(routes, position, x, expert_count, capacity):
    tok_count, width = x.shape
    parts = width // LANES
    return pl.pallas_call(
        functools.partial(place_kernel, capacity),
        out_shape=jax.ShapeDtypeStruct((expert_count * capacity, parts, LANES), jnp.bfloat16),
        in_specs=[SMEM, SMEM, VMEM],
        out_specs=VMEM,
        scratch_shapes=[
            pltpu.VMEM((tok_count * parts, LANES), jnp.float32),
            pltpu.VMEM((tok_count, parts, LANES), jnp.bfloat16),
        ],
        compiler_params=params(),
        name="place_rows",
    )(routes, position, x)


def load_rows(x_ref, step, wide, rows_scr):
    rows = x_ref.shape[0]
    first = step * CHUNK
    wide[...] = x_ref[:, first : first + CHUNK, :].astype(jnp.float32).reshape(rows * CHUNK, LANES)
    for c in range(CHUNK):
        rows_scr[:, c * LANES : (c + 1) * LANES] = wide[pl.ds(c, rows, stride=CHUNK), :].astype(
            jnp.bfloat16
        )


def forward_kernel(x_ref, g0, g1, u0, u1, hidden_ref, slope_ref, active_ref, wide, rows_scr, acc_g, acc_u):
    step = pl.program_id(0)
    steps = x_ref.shape[1] // CHUNK

    @pl.when(step == 0)
    def _():
        acc_g[...] = jnp.zeros_like(acc_g)
        acc_u[...] = jnp.zeros_like(acc_u)

    for s in range(steps):

        @pl.when(step == s)
        def _():
            load_rows(x_ref, s, wide, rows_scr)

    rows = rows_scr[...]
    gate = jnp.concatenate([g0[...], g1[...]], axis=1)
    acc_g[...] += jnp.dot(rows, gate, preferred_element_type=jnp.float32)
    up = jnp.concatenate([u0[...], u1[...]], axis=1)
    acc_u[...] += jnp.dot(rows, up, preferred_element_type=jnp.float32)

    @pl.when(step == steps - 1)
    def _():
        gating = acc_g[...]
        lifted = acc_u[...]
        sigmoid = jax.nn.sigmoid(gating)
        active = gating * sigmoid
        hidden_ref[...] = (active * lifted).astype(jnp.bfloat16)
        slope_ref[...] = lifted * (sigmoid * (1.0 + gating * (1.0 - sigmoid)))
        active_ref[...] = active


def forward_terms(x, g0, g1, u0, u1):
    rows, parts, _ = x.shape
    half = g0.shape[1]
    hid = 2 * half
    depth = CHUNK * LANES
    weight = pl.BlockSpec((depth, half), lambda i: (i, 0))
    whole = pl.BlockSpec((rows, hid), lambda i: (0, 0))
    return pl.pallas_call(
        forward_kernel,
        grid=(parts // CHUNK,),
        out_shape=(
            jax.ShapeDtypeStruct((rows, hid), jnp.bfloat16),
            jax.ShapeDtypeStruct((rows, hid), jnp.float32),
            jax.ShapeDtypeStruct((rows, hid), jnp.float32),
        ),
        in_specs=[VMEM] + [weight] * 4,
        out_specs=(whole, whole, whole),
        scratch_shapes=[
            pltpu.VMEM((rows * CHUNK, LANES), jnp.float32),
            pltpu.VMEM((rows, depth), jnp.bfloat16),
            pltpu.VMEM((rows, hid), jnp.float32),
            pltpu.VMEM((rows, hid), jnp.float32),
        ],
        compiler_params=params(),
        name="forward_terms",
    )(on_chip(x), g0, g1, u0, u1)


def backward_kernel(
    x_ref, d0_hbm, d1_hbm, g0_hbm, g1_hbm, u0_hbm, u1_hbm, hidden_hbm, slope_hbm, active_hbm, out_ref,
    down, gate, up, hidden_ref, slope_ref, active_ref, grads, wide, column, stage, in_sems, out_sems,
):
    contract = (((1,), (1,)), ((), ()))
    rows, parts, _ = x_ref.shape
    steps = parts // CHUNK
    depth = CHUNK * LANES
    half = d0_hbm.shape[0]
    hid = 2 * half
    experts = out_ref.shape[0]
    capacity = rows // experts

    copies = []

    def fetch(src, dst):
        copy = pltpu.make_async_copy(src, dst, in_sems.at[len(copies)])
        copy.start()
        copies.append(copy)
        return copy

    down_in = []
    for step in range(steps):
        cols = pl.ds(step * depth, depth)
        down_in.append(
            [fetch(src.at[:, cols], down.at[step, pl.ds(h * half, half)]) for h, src in enumerate((d0_hbm, d1_hbm))]
        )
    terms_in = [
        fetch(hidden_hbm, hidden_ref), fetch(slope_hbm, slope_ref), fetch(active_hbm, active_ref)
    ]
    weights_in = []
    for step in range(steps):
        part = pl.ds(step * depth, depth)
        weights_in.append(
            [
                fetch(src.at[part], dst.at[h, part])
                for dst, pair in ((gate, (g0_hbm, g1_hbm)), (up, (u0_hbm, u1_hbm)))
                for h, src in enumerate(pair)
            ]
        )

    grad_hidden = None
    for step in range(steps):
        got = x_ref[:, step * CHUNK : (step + 1) * CHUNK, :].reshape(rows, depth)
        for copy in down_in[step]:
            copy.wait()
        total = lax.dot_general(got, down[step], contract, preferred_element_type=jnp.float32)
        grad_hidden = total if step == 0 else grad_hidden + total
    for copy in terms_in:
        copy.wait()
    grads[:, 0:hid] = (grad_hidden * slope_ref[...]).astype(jnp.bfloat16)
    grads[:, hid : 2 * hid] = (grad_hidden * active_ref[...]).astype(jnp.bfloat16)
    prob = jnp.sum(hidden_ref[...].astype(jnp.float32) * grad_hidden, axis=1, keepdims=True)
    column[...] = jnp.broadcast_to(prob, column.shape)
    wide[...] = jnp.zeros_like(wide)
    for s in range(capacity):
        wide[pl.ds(s, experts, stride=CHUNK), :] = column[pl.ds(s, experts, stride=capacity), :]
    stage[:, steps * capacity] = wide[...].reshape(experts, CHUNK, LANES).astype(jnp.bfloat16)

    sends = []

    def send(first, count):
        tiles = pl.ds(first, count)
        copy = pltpu.make_async_copy(
            stage.at[:, tiles], out_ref.at[:, tiles], out_sems.at[len(sends)]
        )
        copy.start()
        sends.append(copy)

    send(steps * capacity, 1)
    for step in range(steps):
        part = pl.ds(step * depth, depth)
        for copy in weights_in[step]:
            copy.wait()
        weight = jnp.concatenate([gate[0, part], gate[1, part], up[0, part], up[1, part]], axis=1)
        total = lax.dot_general(grads[...], weight, contract, preferred_element_type=jnp.float32)
        stage[:, step * capacity : (step + 1) * capacity] = total.astype(jnp.bfloat16).reshape(
            experts, capacity, CHUNK, LANES
        )
        send(step * capacity, capacity)
    for copy in sends:
        copy.wait()


def backward_terms(x, d0, d1, g0, g1, u0, u1, hidden, slope, active, expert_count):
    rows, parts, _ = x.shape
    width, half = g0.shape
    hid = 2 * half
    depth = CHUNK * LANES
    steps = parts // CHUNK
    tiles = rows // expert_count * steps + 1
    anywhere = pl.BlockSpec(memory_space=pl.ANY)
    return pl.pallas_call(
        backward_kernel,
        out_shape=jax.ShapeDtypeStruct((expert_count, tiles, CHUNK, LANES), jnp.bfloat16),
        in_specs=[VMEM] + [anywhere] * 9,
        out_specs=anywhere,
        scratch_shapes=[
            pltpu.VMEM((steps, hid, depth), jnp.bfloat16),
            pltpu.VMEM((2, width, half), jnp.bfloat16),
            pltpu.VMEM((2, width, half), jnp.bfloat16),
            pltpu.VMEM((rows, hid), jnp.bfloat16),
            pltpu.VMEM((rows, hid), jnp.float32),
            pltpu.VMEM((rows, hid), jnp.float32),
            pltpu.VMEM((rows, 2 * hid), jnp.bfloat16),
            pltpu.VMEM((expert_count * CHUNK, LANES), jnp.float32),
            pltpu.VMEM((rows, LANES), jnp.float32),
            pltpu.VMEM((expert_count, tiles, CHUNK, LANES), jnp.bfloat16),
            pltpu.SemaphoreType.DMA((6 * steps + 3,)),
            pltpu.SemaphoreType.DMA((steps + 1,)),
        ],
        compiler_params=params(),
        name="backward_terms",
    )(on_chip(x), d0, d1, g0, g1, u0, u1, hidden, slope, active)


def combine_kernel(capacity, routes_ref, position_ref, probs_ref, back_ref, out_ref, grad_ref, wide):
    top, tok_count = routes_ref.shape
    steps = (back_ref.shape[1] - 1) // capacity
    parts = steps * CHUNK
    sublane = lax.broadcasted_iota(jnp.int32, (CHUNK, LANES), 0)
    lane = lax.broadcasted_iota(jnp.int32, (CHUNK, LANES), 1)

    def gather(t, picked):
        chosen = [(routes_ref[k, t], position_ref[k, t], probs_ref[k, t]) for k in range(top)]
        for step in range(steps):
            total = jnp.zeros((CHUNK, LANES), jnp.float32)
            for e, position, prob in chosen:
                total += prob * back_ref[e, step * capacity + position].astype(jnp.float32)
            wide[pl.ds(pl.multiple_of(t * parts + step * CHUNK, CHUNK), CHUNK), :] = total
        new = []
        for k, (e, position, _) in enumerate(chosen):
            tile = back_ref[e, steps * capacity].astype(jnp.float32)
            here = (sublane == position) & (lane == t)
            new.append(picked[k] + jnp.where(here, tile, 0.0))
        return tuple(new)

    start = tuple(jnp.zeros((CHUNK, LANES), jnp.float32) for _ in range(top))
    picked = lax.fori_loop(0, tok_count, gather, start, unroll=4)
    for k in range(top):
        grad_ref[k : k + 1, :] = jnp.sum(picked[k], axis=0, keepdims=True)
    for c in range(parts):
        out_ref[:, c * LANES : (c + 1) * LANES] = wide[pl.ds(c, tok_count, stride=parts), :].astype(
            jnp.bfloat16
        )


def combine_rows(routes, position, probs, back, capacity):
    top, tok_count = routes.shape
    parts = (back.shape[1] - 1) // capacity * CHUNK
    return pl.pallas_call(
        functools.partial(combine_kernel, capacity),
        out_shape=(
            jax.ShapeDtypeStruct((tok_count, parts * LANES), jnp.bfloat16),
            jax.ShapeDtypeStruct((top, tok_count), jnp.float32),
        ),
        in_specs=[SMEM, SMEM, SMEM, VMEM],
        out_specs=(VMEM, VMEM),
        scratch_shapes=[pltpu.VMEM((tok_count * parts, LANES), jnp.float32)],
        compiler_params=params(),
        name="combine_rows",
    )(routes, position, probs, on_chip(back))


def exchange(blocks, expert_count):
    sent = blocks.reshape(expert_count, -1, blocks.shape[-1])
    got = lax.all_to_all(sent, "expert", split_axis=0, concat_axis=0, tiled=True)
    return got.reshape(blocks.shape)


def on_device(tokens, routes, route_probs, gate_weight, up_weight, down_weight, grad_out):
    tok_count = tokens.shape[0]
    top_count = routes.shape[1]
    expert_count = lax.axis_size("expert")
    capacity = 3 * tok_count * top_count // (2 * expert_count)
    swap = lambda w: lax.ppermute(w, "seq", [(0, 1), (1, 0)])
    gate, up, down = gate_weight[0], up_weight[0], down_weight[0]
    gate_far, up_far, down_far = swap(gate), swap(up), swap(down)
    named = routes.T

    position, send_in = route_and_place(named, tokens, expert_count, capacity)
    recv_in = exchange(send_in, expert_count)
    send_grad = place_rows(named, position, grad_out, expert_count, capacity)
    recv_grad = exchange(send_grad, expert_count)
    hidden, slope, active = forward_terms(recv_in, gate, gate_far, up, up_far)
    out_rows = backward_terms(
        recv_grad, down, down_far, gate, gate_far, up, up_far, hidden, slope, active, expert_count
    )
    back_rows = exchange(out_rows, expert_count)
    grad_tokens, grad_probs = combine_rows(named, position, route_probs.T, back_rows, capacity)
    return (grad_tokens, grad_probs.T.astype(jnp.bfloat16))


def solution(mesh):
    placed = (
        P(("seq", "expert"), None),
        P(("seq", "expert"), None),
        P(("seq", "expert"), None),
        P("expert", None, "seq"),
        P("expert", None, "seq"),
        P("expert", "seq", None),
        P(("seq", "expert"), None),
    )
    return jax.shard_map(
        on_device,
        mesh=mesh,
        in_specs=placed,
        out_specs=(P(("seq", "expert"), None), P(("seq", "expert"), None)),
        check_vma=False,
    )
```

```python
import functools

import jax
import jax.numpy as jnp
from jax import lax
from jax.experimental import pallas as pl
from jax.experimental.pallas import tpu as pltpu
from jax.sharding import PartitionSpec as P

LANES = 128
CHUNK = 8
GROUP = 16
MIB = 1024 * 1024
VMEM = pl.BlockSpec(memory_space=pltpu.VMEM)
SMEM = pl.BlockSpec(memory_space=pltpu.SMEM)
ANYWHERE = pl.BlockSpec(memory_space=pl.ANY)


def params(mib):
    return pltpu.CompilerParams(vmem_limit_bytes=mib * MIB)


def on_chip(x):
    return pltpu.with_memory_space_constraint(x, pltpu.VMEM)


def place_all(routes_ref, position_ref, rows_ref, blocks, stage):
    top, tok_count = routes_ref.shape
    capacity, parts = stage.shape[1:3]
    for r in range(0, tok_count, GROUP):
        blocks[r : r + GROUP] = rows_ref[r : r + GROUP, :].reshape(GROUP, parts, LANES)
    group = 8

    def place(g, _):
        first = g * group
        rows = [blocks[first + i] for i in range(group)]
        targets = [
            [(routes_ref[k, first + i], position_ref[k, first + i]) for k in range(top)]
            for i in range(group)
        ]
        for row, places in zip(rows, targets):
            for e, position in places:
                stage[e, position] = row
        return 0

    lax.fori_loop(0, tok_count // group, place, 0)


def pack_kernel(
    routes_ref, tokens_hbm, grads_hbm, position_ref, out_ref,
    counts, tokens_ref, grads_ref, blocks, stage_in, stage_grad, sems,
):
    top, tok_count = routes_ref.shape
    load_in = pltpu.make_async_copy(tokens_hbm, tokens_ref, sems.at[0])
    load_grad = pltpu.make_async_copy(grads_hbm, grads_ref, sems.at[1])
    load_in.start()
    load_grad.start()

    def clear(e, _):
        counts[e] = 0
        return 0

    lax.fori_loop(0, counts.shape[0], clear, 0, unroll=16)

    def rank(t, _):
        for k in range(top):
            e = routes_ref[k, t]
            position = counts[e]
            counts[e] = position + 1
            position_ref[k, t] = position
        return 0

    lax.fori_loop(0, tok_count, rank, 0, unroll=8)
    load_in.wait()
    place_all(routes_ref, position_ref, tokens_ref, blocks, stage_in)
    send_in = pltpu.make_async_copy(stage_in, out_ref.at[:, 0], sems.at[2])
    send_in.start()
    load_grad.wait()
    place_all(routes_ref, position_ref, grads_ref, blocks, stage_grad)
    send_grad = pltpu.make_async_copy(stage_grad, out_ref.at[:, 1], sems.at[3])
    send_grad.start()
    send_in.wait()
    send_grad.wait()


def pack(routes, tokens, grads, expert_count, capacity):
    tok_count, width = tokens.shape
    parts = width // LANES
    stage = pltpu.VMEM((expert_count, capacity, parts, LANES), jnp.bfloat16)
    return pl.pallas_call(
        pack_kernel,
        out_shape=(
            jax.ShapeDtypeStruct(routes.shape, jnp.int32),
            jax.ShapeDtypeStruct((expert_count, 2, capacity, parts, LANES), jnp.bfloat16),
        ),
        in_specs=[SMEM, ANYWHERE, ANYWHERE],
        out_specs=(SMEM, ANYWHERE),
        scratch_shapes=[
            pltpu.SMEM((expert_count,), jnp.int32),
            pltpu.VMEM((tok_count, width), jnp.bfloat16),
            pltpu.VMEM((tok_count, width), jnp.bfloat16),
            pltpu.VMEM((tok_count, parts, LANES), jnp.bfloat16),
            stage,
            stage,
            pltpu.SemaphoreType.DMA((4,)),
        ],
        compiler_params=params(62),
        name="pack",
    )(routes, tokens, grads)


def expert_kernel(
    x_hbm, d0_hbm, d1_hbm, g0_hbm, g1_hbm, u0_hbm, u1_hbm, out_ref,
    x_ref, down, gate_up, grads, wide, column, stage, in_sems, out_sems,
):
    contract = (((1,), (1,)), ((), ()))
    experts, _, capacity, parts, _ = x_hbm.shape
    rows = experts * capacity
    steps = parts // CHUNK
    depth = CHUNK * LANES
    half = d0_hbm.shape[0]
    hid = 2 * half

    fetches = []

    def fetch(src, dst):
        copy = pltpu.make_async_copy(src, dst, in_sems.at[len(fetches)])
        copy.start()
        fetches.append(copy)
        return copy

    def cut(step):
        return pl.ds(step * depth, depth)

    def fetch_rows(which, step):
        return fetch(
            x_hbm.at[:, which, :, pl.ds(step * CHUNK, CHUNK)], x_ref.at[which, step]
        )

    gate_up_in = [
        [fetch_rows(0, step)]
        + [
            fetch(src.at[cut(step)], gate_up.at[cut(step), pl.ds(h * half, half)])
            for h, src in enumerate((g0_hbm, g1_hbm, u0_hbm, u1_hbm))
        ]
        for step in range(steps)
    ]
    down_in = [
        [fetch_rows(1, step)]
        + [
            fetch(src.at[:, cut(step)], down.at[pl.ds(h * half, half), cut(step)])
            for h, src in enumerate((d0_hbm, d1_hbm))
        ]
        for step in range(steps)
    ]

    def taken(which, step):
        return x_ref[which, step].reshape(rows, CHUNK, LANES).reshape(rows, depth)

    both = None
    for step in range(steps):
        for copy in gate_up_in[step]:
            copy.wait()
        part = jnp.dot(taken(0, step), gate_up[cut(step)], preferred_element_type=jnp.float32)
        both = part if step == 0 else both + part
    wide[...] = both

    grad_hidden = None
    for step in range(steps):
        for copy in down_in[step]:
            copy.wait()
        part = lax.dot_general(
            taken(1, step), down[:, cut(step)], contract, preferred_element_type=jnp.float32
        )
        grad_hidden = part if step == 0 else grad_hidden + part

    gating = wide[:, 0:hid]
    lifted = wide[:, hid : 2 * hid]
    sigmoid = jax.nn.sigmoid(gating)
    active = gating * sigmoid
    hidden = (active * lifted).astype(jnp.bfloat16)
    slope = sigmoid * (1.0 + gating * (1.0 - sigmoid))
    grads[:, 0:hid] = (grad_hidden * lifted * slope).astype(jnp.bfloat16)
    grads[:, hid : 2 * hid] = (grad_hidden * active).astype(jnp.bfloat16)
    prob = jnp.sum(hidden.astype(jnp.float32) * grad_hidden, axis=1, keepdims=True)
    column[0:rows, :] = jnp.broadcast_to(prob, (rows, LANES))

    sends = []

    def send(tile):
        copy = pltpu.make_async_copy(stage.at[:, tile], out_ref.at[:, tile], out_sems.at[len(sends)])
        copy.start()
        sends.append(copy)

    for step in range(steps):
        part = lax.dot_general(
            grads[...], gate_up[cut(step)], contract, preferred_element_type=jnp.float32
        )
        tiles = part.astype(jnp.bfloat16).reshape(experts, capacity, CHUNK, LANES)
        for s in range(capacity):
            stage[:, s * steps + step] = tiles[:, s]
            send(s * steps + step)
        if step == 0:
            picked = [column[pl.ds(s, experts, stride=capacity), :] for s in range(capacity)]
            column[0 : experts * CHUNK, :] = jnp.zeros((experts * CHUNK, LANES), jnp.float32)
            for s in range(capacity):
                column[pl.ds(s, experts, stride=CHUNK), :] = picked[s]
            stage[:, capacity * steps] = (
                column[0 : experts * CHUNK, :].reshape(experts, CHUNK, LANES).astype(jnp.bfloat16)
            )
            send(capacity * steps)
    for copy in sends:
        copy.wait()


def expert_terms(x, d0, d1, g0, g1, u0, u1):
    expert_count, _, capacity, parts, _ = x.shape
    rows = expert_count * capacity
    width, half = g0.shape
    hid = 2 * half
    steps = parts // CHUNK
    tiles = capacity * steps + 1
    return pl.pallas_call(
        expert_kernel,
        out_shape=jax.ShapeDtypeStruct((expert_count, tiles, CHUNK, LANES), jnp.bfloat16),
        in_specs=[ANYWHERE] * 7,
        out_specs=ANYWHERE,
        scratch_shapes=[
            pltpu.VMEM((2, steps, expert_count, capacity, CHUNK, LANES), jnp.bfloat16),
            pltpu.VMEM((hid, width), jnp.bfloat16),
            pltpu.VMEM((width, 2 * hid), jnp.bfloat16),
            pltpu.VMEM((rows, 2 * hid), jnp.bfloat16),
            pltpu.VMEM((rows, 2 * hid), jnp.float32),
            pltpu.VMEM((max(rows, expert_count * CHUNK), LANES), jnp.float32),
            pltpu.VMEM((expert_count, tiles, CHUNK, LANES), jnp.bfloat16),
            pltpu.SemaphoreType.DMA((8 * steps,)),
            pltpu.SemaphoreType.DMA((tiles,)),
        ],
        compiler_params=params(62),
        name="expert_terms",
    )(x, d0, d1, g0, g1, u0, u1)


def combine_kernel(routes_ref, position_ref, probs_ref, back_ref, out_ref, grad_ref, blocks):
    top, tok_count = routes_ref.shape
    parts = blocks.shape[1]
    steps = parts // CHUNK
    last = back_ref.shape[1] - 1
    group = 4
    sublane = lax.broadcasted_iota(jnp.int32, (CHUNK, LANES), 0)
    lane = lax.broadcasted_iota(jnp.int32, (CHUNK, LANES), 1)

    def gather(g, picked):
        picked = list(picked)
        rows = []
        for i in range(group):
            t = g * group + i
            total = None
            for k in range(top):
                e, position = routes_ref[k, t], position_ref[k, t]
                row = back_ref[e, pl.ds(position * steps, steps)].reshape(parts, LANES)
                term = probs_ref[k, t] * row.astype(jnp.float32)
                total = term if k == 0 else total + term
                tile = back_ref[e, last].astype(jnp.float32)
                here = (sublane == position) & (lane == t)
                picked[k] = jnp.where(here, tile, picked[k])
            rows.append(total.astype(jnp.bfloat16))
        for i in range(group):
            blocks[g * group + i] = rows[i]
        return tuple(picked)

    start = tuple(jnp.zeros((CHUNK, LANES), jnp.float32) for _ in range(top))
    picked = lax.fori_loop(0, tok_count // group, gather, start)
    grad_ref[...] = jnp.concatenate(
        [jnp.sum(p, axis=0, keepdims=True) for p in picked], axis=0
    ).astype(jnp.bfloat16)
    for r in range(0, tok_count, GROUP):
        out_ref[r : r + GROUP, :] = blocks[r : r + GROUP].reshape(GROUP, parts * LANES)


def combine(routes, position, probs, back, width):
    top, tok_count = routes.shape
    return pl.pallas_call(
        combine_kernel,
        out_shape=(
            jax.ShapeDtypeStruct((tok_count, width), jnp.bfloat16),
            jax.ShapeDtypeStruct((top, tok_count), jnp.bfloat16),
        ),
        in_specs=[SMEM, SMEM, SMEM, VMEM],
        out_specs=(VMEM, VMEM),
        scratch_shapes=[pltpu.VMEM((tok_count, width // LANES, LANES), jnp.bfloat16)],
        compiler_params=params(56),
        name="combine",
    )(routes, position, probs, on_chip(back))


def exchange(blocks):
    sent = blocks.reshape(blocks.shape[0], -1, blocks.shape[-1])
    got = lax.all_to_all(sent, "expert", split_axis=0, concat_axis=0, tiled=True)
    return got.reshape(blocks.shape)


def on_device(tokens, routes, route_probs, gate_weight, up_weight, down_weight, grad_out):
    tok_count, width = tokens.shape
    top_count = routes.shape[1]
    expert_count = lax.axis_size("expert")
    capacity = 3 * tok_count * top_count // (2 * expert_count)
    swap = lambda w: lax.ppermute(w, "seq", [(0, 1), (1, 0)])
    gate, up, down = gate_weight[0], up_weight[0], down_weight[0]
    gate_far, up_far, down_far = swap(gate), swap(up), swap(down)
    named = routes.T

    position, sent = pack(named, tokens, grad_out, expert_count, capacity)
    received = exchange(sent)
    rows = expert_terms(received, down, down_far, gate, gate_far, up, up_far)
    back = exchange(rows)
    grad_tokens, grad_probs = combine(named, position, route_probs.T, back, width)
    return (grad_tokens, grad_probs.T)


def solution(mesh):
    placed = (
        P(("seq", "expert"), None),
        P(("seq", "expert"), None),
        P(("seq", "expert"), None),
        P("expert", None, "seq"),
        P("expert", None, "seq"),
        P("expert", "seq", None),
        P(("seq", "expert"), None),
    )
    return jax.shard_map(
        on_device,
        mesh=mesh,
        in_specs=placed,
        out_specs=(P(("seq", "expert"), None), P(("seq", "expert"), None)),
        check_vma=False,
    )
```

```python
import functools

import jax
import jax.numpy as jnp
from jax import lax
from jax.experimental import pallas as pl
from jax.experimental.pallas import tpu as pltpu
from jax.sharding import PartitionSpec as P

LANES = 128
CHUNK = 8
GROUP = 16
AHEAD = 8
BLOCKS = 1
MIB = 1024 * 1024
VMEM = pl.BlockSpec(memory_space=pltpu.VMEM)
SMEM = pl.BlockSpec(memory_space=pltpu.SMEM)
ANYWHERE = pl.BlockSpec(memory_space=pl.ANY)


def params(mib):
    return pltpu.CompilerParams(vmem_limit_bytes=mib * MIB)


def on_chip(x):
    return pltpu.with_memory_space_constraint(x, pltpu.VMEM)


def place_rows(rows_ref, stage, slots_of):
    tok_count = rows_ref.shape[0]
    parts = stage.shape[2]

    def place(g, _):
        first = pl.multiple_of(g * GROUP, GROUP)
        rows = rows_ref[pl.ds(first, GROUP), :].reshape(GROUP, parts, LANES)
        for i in range(GROUP):
            for e, position in slots_of(first + i):
                stage[e, position] = rows[i]
        return 0

    lax.fori_loop(0, tok_count // GROUP, place, 0)


def pack_kernel(
    routes_ref, tokens_hbm, grads_hbm, position_ref, out_ref,
    counts, tokens_ref, grads_ref, stage_in, stage_grad, sems,
):
    top = routes_ref.shape[0]
    load_in = pltpu.make_async_copy(tokens_hbm, tokens_ref, sems.at[0])
    load_grad = pltpu.make_async_copy(grads_hbm, grads_ref, sems.at[1])
    load_in.start()
    load_grad.start()

    def clear(e, _):
        counts[e] = 0
        return 0

    lax.fori_loop(0, counts.shape[0], clear, 0, unroll=16)

    def ranked(t):
        slots = []
        for k in range(top):
            e = routes_ref[k, t]
            position = counts[e]
            counts[e] = position + 1
            position_ref[k, t] = position
            slots.append((e, position))
        return slots

    def known(t):
        return [(routes_ref[k, t], position_ref[k, t]) for k in range(top)]

    load_in.wait()
    place_rows(tokens_ref, stage_in, ranked)
    send_in = pltpu.make_async_copy(stage_in, out_ref.at[:, 0], sems.at[2])
    send_in.start()
    load_grad.wait()
    place_rows(grads_ref, stage_grad, known)
    send_grad = pltpu.make_async_copy(stage_grad, out_ref.at[:, 1], sems.at[3])
    send_grad.start()
    send_in.wait()
    send_grad.wait()


def pack(routes, tokens, grads, expert_count, capacity):
    tok_count, width = tokens.shape
    parts = width // LANES
    stage = pltpu.VMEM((expert_count, capacity, parts, LANES), jnp.bfloat16)
    return pl.pallas_call(
        pack_kernel,
        out_shape=(
            jax.ShapeDtypeStruct(routes.shape, jnp.int32),
            jax.ShapeDtypeStruct((expert_count, 2, capacity, parts, LANES), jnp.bfloat16),
        ),
        in_specs=[SMEM, ANYWHERE, ANYWHERE],
        out_specs=(SMEM, ANYWHERE),
        scratch_shapes=[
            pltpu.SMEM((expert_count,), jnp.int32),
            pltpu.VMEM((tok_count, width), jnp.bfloat16),
            pltpu.VMEM((tok_count, width), jnp.bfloat16),
            stage,
            stage,
            pltpu.SemaphoreType.DMA((4,)),
        ],
        compiler_params=params(62),
        name="pack",
    )(routes, tokens, grads)


def expert_kernel(
    x_hbm, d0_hbm, d1_hbm, g0_hbm, g1_hbm, u0_hbm, u1_hbm, out_ref,
    x_ref, down, gate_up, grads, wide, column, stage, in_sems, out_sems,
):
    contract = (((1,), (1,)), ((), ()))
    experts, _, capacity, parts, _ = x_hbm.shape
    rows = experts * capacity
    steps = parts // CHUNK
    depth = CHUNK * LANES
    half = d0_hbm.shape[0]
    hid = 2 * half
    dests = experts // BLOCKS
    some = dests * capacity

    def cut(step):
        return pl.ds(step * depth, depth)

    count = [0]

    def fetch(src, dst):
        count[0] += 1
        return pltpu.make_async_copy(src, dst, in_sems.at[count[0] - 1])

    def fetch_rows(which, step):
        return fetch(x_hbm.at[:, which, :, pl.ds(step * CHUNK, CHUNK)], x_ref.at[which, step])

    batches = [
        [fetch_rows(0, step)]
        + [
            fetch(src.at[cut(step)], gate_up.at[cut(step), pl.ds(h * half, half)])
            for h, src in enumerate((g0_hbm, g1_hbm, u0_hbm, u1_hbm))
        ]
        for step in range(steps)
    ] + [
        [fetch_rows(1, step)]
        + [
            fetch(src.at[:, cut(step)], down.at[pl.ds(h * half, half), cut(step)])
            for h, src in enumerate((d0_hbm, d1_hbm))
        ]
        for step in range(steps)
    ]
    for batch in batches[:AHEAD]:
        for copy in batch:
            copy.start()

    def arrive(i):
        for copy in batches[i]:
            copy.wait()
        for batch in batches[i + AHEAD : i + AHEAD + 1]:
            for copy in batch:
                copy.start()

    def taken(which, step, first, number):
        part = x_ref[which, step, first : first + number]
        return part.reshape(number * capacity, CHUNK, LANES).reshape(number * capacity, depth)

    both = None
    for step in range(steps):
        arrive(step)
        part = jnp.dot(
            taken(0, step, 0, experts), gate_up[cut(step)], preferred_element_type=jnp.float32
        )
        both = part if step == 0 else both + part
    wide[...] = both
    for step in range(steps):
        arrive(steps + step)

    for b in range(BLOCKS):
        here = slice(b * some, (b + 1) * some)
        grad_hidden = None
        for step in range(steps):
            part = lax.dot_general(
                taken(1, step, b * dests, dests),
                down[:, cut(step)],
                contract,
                preferred_element_type=jnp.float32,
            )
            grad_hidden = part if step == 0 else grad_hidden + part
        gating = wide[here, 0:hid]
        lifted = wide[here, hid : 2 * hid]
        sigmoid = jax.nn.sigmoid(gating)
        active = gating * sigmoid
        hidden = (active * lifted).astype(jnp.bfloat16)
        slope = sigmoid * (1.0 + gating * (1.0 - sigmoid))
        grads[here, 0:hid] = (grad_hidden * lifted * slope).astype(jnp.bfloat16)
        grads[here, hid : 2 * hid] = (grad_hidden * active).astype(jnp.bfloat16)
        prob = jnp.sum(hidden.astype(jnp.float32) * grad_hidden, axis=1, keepdims=True)
        column[here, :] = jnp.broadcast_to(prob, (some, LANES))

    sends = []

    def send(first, number, tile):
        places = pl.ds(first, number)
        copy = pltpu.make_async_copy(
            stage.at[places, tile], out_ref.at[places, tile], out_sems.at[len(sends)]
        )
        copy.start()
        sends.append(copy)

    for b in range(BLOCKS):
        for step in range(steps):
            part = lax.dot_general(
                grads[b * some : (b + 1) * some, :],
                gate_up[cut(step)],
                contract,
                preferred_element_type=jnp.float32,
            )
            tiles = part.astype(jnp.bfloat16).reshape(dests, capacity, CHUNK, LANES)
            for s in range(capacity):
                stage[b * dests : (b + 1) * dests, s * steps + step] = tiles[:, s]
            if b == 0 and step == 0:
                picked = [column[pl.ds(s, experts, stride=capacity), :] for s in range(capacity)]
                column[0 : experts * CHUNK, :] = jnp.zeros((experts * CHUNK, LANES), jnp.float32)
                for s in range(capacity):
                    column[pl.ds(s, experts, stride=CHUNK), :] = picked[s]
                stage[:, capacity * steps] = (
                    column[0 : experts * CHUNK, :].reshape(experts, CHUNK, LANES).astype(jnp.bfloat16)
                )
                send(0, experts, capacity * steps)
            for s in range(capacity):
                send(b * dests, dests, s * steps + step)
    for copy in sends:
        copy.wait()


def expert_terms(x, d0, d1, g0, g1, u0, u1):
    expert_count, _, capacity, parts, _ = x.shape
    rows = expert_count * capacity
    width, half = g0.shape
    hid = 2 * half
    steps = parts // CHUNK
    tiles = capacity * steps + 1
    return pl.pallas_call(
        expert_kernel,
        out_shape=jax.ShapeDtypeStruct((expert_count, tiles, CHUNK, LANES), jnp.bfloat16),
        in_specs=[ANYWHERE] * 7,
        out_specs=ANYWHERE,
        scratch_shapes=[
            pltpu.VMEM((2, steps, expert_count, capacity, CHUNK, LANES), jnp.bfloat16),
            pltpu.VMEM((hid, width), jnp.bfloat16),
            pltpu.VMEM((width, 2 * hid), jnp.bfloat16),
            pltpu.VMEM((rows, 2 * hid), jnp.bfloat16),
            pltpu.VMEM((rows, 2 * hid), jnp.float32),
            pltpu.VMEM((max(rows, expert_count * CHUNK), LANES), jnp.float32),
            pltpu.VMEM((expert_count, tiles, CHUNK, LANES), jnp.bfloat16),
            pltpu.SemaphoreType.DMA((8 * steps,)),
            pltpu.SemaphoreType.DMA((BLOCKS * (tiles - 1) + 1,)),
        ],
        compiler_params=params(50),
        name="expert_terms",
    )(x, d0, d1, g0, g1, u0, u1)


def combine_kernel(routes_ref, position_ref, probs_ref, back_ref, out_ref, grad_ref, blocks):
    top, tok_count = routes_ref.shape
    parts = blocks.shape[1]
    steps = parts // CHUNK
    last = back_ref.shape[1] - 1
    group = 4
    sublane = lax.broadcasted_iota(jnp.int32, (CHUNK, LANES), 0)
    lane = lax.broadcasted_iota(jnp.int32, (CHUNK, LANES), 1)

    def gather(g, picked):
        picked = list(picked)
        rows = []
        for i in range(group):
            t = g * group + i
            total = None
            for k in range(top):
                e, position = routes_ref[k, t], position_ref[k, t]
                row = back_ref[e, pl.ds(position * steps, steps)].reshape(parts, LANES)
                term = probs_ref[k, t] * row.astype(jnp.float32)
                total = term if k == 0 else total + term
                tile = back_ref[e, last].astype(jnp.float32)
                here = (sublane == position) & (lane == t)
                picked[k] = jnp.where(here, tile, picked[k])
            rows.append(total.astype(jnp.bfloat16))
        for i in range(group):
            blocks[g * group + i] = rows[i]
        return tuple(picked)

    start = tuple(jnp.zeros((CHUNK, LANES), jnp.float32) for _ in range(top))
    picked = lax.fori_loop(0, tok_count // group, gather, start)
    grad_ref[...] = jnp.concatenate(
        [jnp.sum(p, axis=0, keepdims=True) for p in picked], axis=0
    ).astype(jnp.bfloat16)
    for r in range(0, tok_count, GROUP):
        out_ref[r : r + GROUP, :] = blocks[r : r + GROUP].reshape(GROUP, parts * LANES)


def combine(routes, position, probs, back, width):
    top, tok_count = routes.shape
    return pl.pallas_call(
        combine_kernel,
        out_shape=(
            jax.ShapeDtypeStruct((tok_count, width), jnp.bfloat16),
            jax.ShapeDtypeStruct((top, tok_count), jnp.bfloat16),
        ),
        in_specs=[SMEM, SMEM, SMEM, VMEM],
        out_specs=(VMEM, VMEM),
        scratch_shapes=[pltpu.VMEM((tok_count, width // LANES, LANES), jnp.bfloat16)],
        compiler_params=params(56),
        name="combine",
    )(routes, position, probs, on_chip(back))


def exchange(blocks):
    sent = blocks.reshape(blocks.shape[0], -1, blocks.shape[-1])
    got = lax.all_to_all(sent, "expert", split_axis=0, concat_axis=0, tiled=True)
    return got.reshape(blocks.shape)


def on_device(tokens, routes, route_probs, gate_weight, up_weight, down_weight, grad_out):
    tok_count, width = tokens.shape
    top_count = routes.shape[1]
    expert_count = lax.axis_size("expert")
    capacity = 3 * tok_count * top_count // (2 * expert_count)
    swap = lambda w: lax.ppermute(w, "seq", [(0, 1), (1, 0)])
    gate, up, down = gate_weight[0], up_weight[0], down_weight[0]
    gate_far, up_far, down_far = swap(gate), swap(up), swap(down)
    named = routes.T

    position, sent = pack(named, tokens, grad_out, expert_count, capacity)
    received = exchange(sent)
    rows = expert_terms(received, down, down_far, gate, gate_far, up, up_far)
    back = exchange(rows)
    grad_tokens, grad_probs = combine(named, position, route_probs.T, back, width)
    return (grad_tokens, grad_probs.T)


def solution(mesh):
    placed = (
        P(("seq", "expert"), None),
        P(("seq", "expert"), None),
        P(("seq", "expert"), None),
        P("expert", None, "seq"),
        P("expert", None, "seq"),
        P("expert", "seq", None),
        P(("seq", "expert"), None),
    )
    return jax.shard_map(
        on_device,
        mesh=mesh,
        in_specs=placed,
        out_specs=(P(("seq", "expert"), None), P(("seq", "expert"), None)),
        check_vma=False,
    )
```

```python
import functools

import jax
import jax.numpy as jnp
from jax import lax
from jax.experimental import pallas as pl
from jax.experimental.pallas import tpu as pltpu
from jax.sharding import PartitionSpec as P

LANES = 128
CHUNK = 8
GROUP = 16
AHEAD = 8
BLOCKS = 1
PIECES = 4
MIB = 1024 * 1024
VMEM = pl.BlockSpec(memory_space=pltpu.VMEM)
SMEM = pl.BlockSpec(memory_space=pltpu.SMEM)
ANYWHERE = pl.BlockSpec(memory_space=pl.ANY)


def params(mib):
    return pltpu.CompilerParams(vmem_limit_bytes=mib * MIB)


def on_chip(x):
    return pltpu.with_memory_space_constraint(x, pltpu.VMEM)


def place_rows(rows_ref, source, blocks, stage, send):
    tok_count = rows_ref.shape[0]
    experts, capacity, parts, _ = stage.shape
    for r in range(0, tok_count, GROUP):
        blocks[r : r + GROUP] = rows_ref[r : r + GROUP, :].reshape(GROUP, parts, LANES)
    group = 4
    share = experts // PIECES

    def place(g, _):
        first = g * group
        rows = [
            [blocks[source[(first + i) * capacity + s]] for s in range(capacity)]
            for i in range(group)
        ]
        for i in range(group):
            for s in range(capacity):
                stage[first + i, s] = rows[i][s]
        return 0

    for piece in range(PIECES):
        lax.fori_loop(piece * share // group, (piece + 1) * share // group, place, 0)
        send(piece, pl.ds(piece * share, share))


def pack_kernel(
    routes_ref, tokens_hbm, grads_hbm, position_ref, out_ref,
    counts, source, tokens_ref, grads_ref, blocks, stage_in, stage_grad, sems,
):
    top, tok_count = routes_ref.shape
    capacity = stage_in.shape[1]
    load_in = pltpu.make_async_copy(tokens_hbm, tokens_ref, sems.at[0])
    load_grad = pltpu.make_async_copy(grads_hbm, grads_ref, sems.at[1])
    load_in.start()
    load_grad.start()

    def clear(e, _):
        counts[e] = 0
        for s in range(capacity):
            source[e * capacity + s] = 0
        return 0

    lax.fori_loop(0, counts.shape[0], clear, 0, unroll=8)

    def rank(t, _):
        for k in range(top):
            e = routes_ref[k, t]
            position = counts[e]
            counts[e] = position + 1
            position_ref[k, t] = position
            source[e * capacity + position] = t
        return 0

    lax.fori_loop(0, tok_count, rank, 0, unroll=8)
    sends = []

    def sender(stage, which):
        def send(piece, some):
            copy = pltpu.make_async_copy(
                stage.at[some], out_ref.at[some, which], sems.at[2 + which * PIECES + piece]
            )
            copy.start()
            sends.append(copy)

        return send

    load_in.wait()
    place_rows(tokens_ref, source, blocks, stage_in, sender(stage_in, 0))
    load_grad.wait()
    place_rows(grads_ref, source, blocks, stage_grad, sender(stage_grad, 1))
    for copy in sends:
        copy.wait()


def pack(routes, tokens, grads, expert_count, capacity):
    tok_count, width = tokens.shape
    parts = width // LANES
    stage = pltpu.VMEM((expert_count, capacity, parts, LANES), jnp.bfloat16)
    return pl.pallas_call(
        pack_kernel,
        out_shape=(
            jax.ShapeDtypeStruct(routes.shape, jnp.int32),
            jax.ShapeDtypeStruct((expert_count, 2, capacity, parts, LANES), jnp.bfloat16),
        ),
        in_specs=[SMEM, ANYWHERE, ANYWHERE],
        out_specs=(SMEM, ANYWHERE),
        scratch_shapes=[
            pltpu.SMEM((expert_count,), jnp.int32),
            pltpu.SMEM((expert_count * capacity,), jnp.int32),
            pltpu.VMEM((tok_count, width), jnp.bfloat16),
            pltpu.VMEM((tok_count, width), jnp.bfloat16),
            pltpu.VMEM((tok_count, parts, LANES), jnp.bfloat16),
            stage,
            stage,
            pltpu.SemaphoreType.DMA((2 + 2 * PIECES,)),
        ],
        compiler_params=params(62),
        name="pack",
    )(routes, tokens, grads)


def expert_kernel(
    x_hbm, d0_hbm, d1_hbm, g0_hbm, g1_hbm, u0_hbm, u1_hbm, out_ref,
    x_ref, down, gate_up, grads, wide, column, stage, in_sems, out_sems,
):
    contract = (((1,), (1,)), ((), ()))
    experts, _, capacity, parts, _ = x_hbm.shape
    rows = experts * capacity
    steps = parts // CHUNK
    depth = CHUNK * LANES
    half = d0_hbm.shape[0]
    hid = 2 * half
    dests = experts // BLOCKS
    some = dests * capacity

    def cut(step):
        return pl.ds(step * depth, depth)

    count = [0]

    def fetch(src, dst):
        count[0] += 1
        return pltpu.make_async_copy(src, dst, in_sems.at[count[0] - 1])

    def fetch_rows(which, step):
        return fetch(x_hbm.at[:, which, :, pl.ds(step * CHUNK, CHUNK)], x_ref.at[which, step])

    batches = [
        [fetch_rows(0, step)]
        + [
            fetch(src.at[cut(step)], gate_up.at[cut(step), pl.ds(h * half, half)])
            for h, src in enumerate((g0_hbm, g1_hbm, u0_hbm, u1_hbm))
        ]
        for step in range(steps)
    ] + [
        [fetch_rows(1, step)]
        + [
            fetch(src.at[:, cut(step)], down.at[pl.ds(h * half, half), cut(step)])
            for h, src in enumerate((d0_hbm, d1_hbm))
        ]
        for step in range(steps)
    ]
    for batch in batches[:AHEAD]:
        for copy in batch:
            copy.start()

    def arrive(i):
        for copy in batches[i]:
            copy.wait()
        for batch in batches[i + AHEAD : i + AHEAD + 1]:
            for copy in batch:
                copy.start()

    def taken(which, step, first, number):
        part = x_ref[which, step, first : first + number]
        return part.reshape(number * capacity, CHUNK, LANES).reshape(number * capacity, depth)

    both = None
    for step in range(steps):
        arrive(step)
        part = jnp.dot(
            taken(0, step, 0, experts), gate_up[cut(step)], preferred_element_type=jnp.float32
        )
        both = part if step == 0 else both + part
    wide[...] = both
    for step in range(steps):
        arrive(steps + step)

    for b in range(BLOCKS):
        here = slice(b * some, (b + 1) * some)
        grad_hidden = None
        for step in range(steps):
            part = lax.dot_general(
                taken(1, step, b * dests, dests),
                down[:, cut(step)],
                contract,
                preferred_element_type=jnp.float32,
            )
            grad_hidden = part if step == 0 else grad_hidden + part
        gating = wide[here, 0:hid]
        lifted = wide[here, hid : 2 * hid]
        sigmoid = jax.nn.sigmoid(gating)
        active = gating * sigmoid
        hidden = (active * lifted).astype(jnp.bfloat16)
        slope = sigmoid * (1.0 + gating * (1.0 - sigmoid))
        grads[here, 0:hid] = (grad_hidden * lifted * slope).astype(jnp.bfloat16)
        grads[here, hid : 2 * hid] = (grad_hidden * active).astype(jnp.bfloat16)
        prob = jnp.sum(hidden.astype(jnp.float32) * grad_hidden, axis=1, keepdims=True)
        column[here, :] = jnp.broadcast_to(prob, (some, LANES))

    sends = []

    def send(first, number, tile):
        places = pl.ds(first, number)
        copy = pltpu.make_async_copy(
            stage.at[places, tile], out_ref.at[places, tile], out_sems.at[len(sends)]
        )
        copy.start()
        sends.append(copy)

    for b in range(BLOCKS):
        for step in range(steps):
            part = lax.dot_general(
                grads[b * some : (b + 1) * some, :],
                gate_up[cut(step)],
                contract,
                preferred_element_type=jnp.float32,
            )
            tiles = part.astype(jnp.bfloat16).reshape(dests, capacity, CHUNK, LANES)
            for s in range(capacity):
                stage[b * dests : (b + 1) * dests, s * steps + step] = tiles[:, s]
            if b == 0 and step == 0:
                picked = [column[pl.ds(s, experts, stride=capacity), :] for s in range(capacity)]
                column[0 : experts * CHUNK, :] = jnp.zeros((experts * CHUNK, LANES), jnp.float32)
                for s in range(capacity):
                    column[pl.ds(s, experts, stride=CHUNK), :] = picked[s]
                stage[:, capacity * steps] = (
                    column[0 : experts * CHUNK, :].reshape(experts, CHUNK, LANES).astype(jnp.bfloat16)
                )
                send(0, experts, capacity * steps)
            for s in range(capacity):
                send(b * dests, dests, s * steps + step)
    for copy in sends:
        copy.wait()


def expert_terms(x, d0, d1, g0, g1, u0, u1):
    expert_count, _, capacity, parts, _ = x.shape
    rows = expert_count * capacity
    width, half = g0.shape
    hid = 2 * half
    steps = parts // CHUNK
    tiles = capacity * steps + 1
    return pl.pallas_call(
        expert_kernel,
        out_shape=jax.ShapeDtypeStruct((expert_count, tiles, CHUNK, LANES), jnp.bfloat16),
        in_specs=[ANYWHERE] * 7,
        out_specs=ANYWHERE,
        scratch_shapes=[
            pltpu.VMEM((2, steps, expert_count, capacity, CHUNK, LANES), jnp.bfloat16),
            pltpu.VMEM((hid, width), jnp.bfloat16),
            pltpu.VMEM((width, 2 * hid), jnp.bfloat16),
            pltpu.VMEM((rows, 2 * hid), jnp.bfloat16),
            pltpu.VMEM((rows, 2 * hid), jnp.float32),
            pltpu.VMEM((max(rows, expert_count * CHUNK), LANES), jnp.float32),
            pltpu.VMEM((expert_count, tiles, CHUNK, LANES), jnp.bfloat16),
            pltpu.SemaphoreType.DMA((8 * steps,)),
            pltpu.SemaphoreType.DMA((BLOCKS * (tiles - 1) + 1,)),
        ],
        compiler_params=params(50),
        name="expert_terms",
    )(x, d0, d1, g0, g1, u0, u1)


def combine_kernel(routes_ref, position_ref, probs_ref, back_ref, out_ref, grad_ref, blocks):
    top, tok_count = routes_ref.shape
    parts = blocks.shape[1]
    steps = parts // CHUNK
    last = back_ref.shape[1] - 1
    group = 4
    sublane = lax.broadcasted_iota(jnp.int32, (CHUNK, LANES), 0)
    lane = lax.broadcasted_iota(jnp.int32, (CHUNK, LANES), 1)

    def gather(g, picked):
        picked = list(picked)
        rows = []
        for i in range(group):
            t = g * group + i
            total = None
            for k in range(top):
                e, position = routes_ref[k, t], position_ref[k, t]
                row = back_ref[e, pl.ds(position * steps, steps)].reshape(parts, LANES)
                term = probs_ref[k, t] * row.astype(jnp.float32)
                total = term if k == 0 else total + term
                tile = back_ref[e, last].astype(jnp.float32)
                here = (sublane == position) & (lane == t)
                picked[k] = jnp.where(here, tile, picked[k])
            rows.append(total.astype(jnp.bfloat16))
        for i in range(group):
            blocks[g * group + i] = rows[i]
        return tuple(picked)

    start = tuple(jnp.zeros((CHUNK, LANES), jnp.float32) for _ in range(top))
    picked = lax.fori_loop(0, tok_count // group, gather, start)
    grad_ref[...] = jnp.concatenate(
        [jnp.sum(p, axis=0, keepdims=True) for p in picked], axis=0
    ).astype(jnp.bfloat16)
    for r in range(0, tok_count, GROUP):
        out_ref[r : r + GROUP, :] = blocks[r : r + GROUP].reshape(GROUP, parts * LANES)


def combine(routes, position, probs, back, width):
    top, tok_count = routes.shape
    return pl.pallas_call(
        combine_kernel,
        out_shape=(
            jax.ShapeDtypeStruct((tok_count, width), jnp.bfloat16),
            jax.ShapeDtypeStruct((top, tok_count), jnp.bfloat16),
        ),
        in_specs=[SMEM, SMEM, SMEM, VMEM],
        out_specs=(VMEM, VMEM),
        scratch_shapes=[pltpu.VMEM((tok_count, width // LANES, LANES), jnp.bfloat16)],
        compiler_params=params(56),
        name="combine",
    )(routes, position, probs, on_chip(back))


def exchange(blocks):
    sent = blocks.reshape(blocks.shape[0], -1, blocks.shape[-1])
    got = lax.all_to_all(sent, "expert", split_axis=0, concat_axis=0, tiled=True)
    return got.reshape(blocks.shape)


def on_device(tokens, routes, route_probs, gate_weight, up_weight, down_weight, grad_out):
    tok_count, width = tokens.shape
    top_count = routes.shape[1]
    expert_count = lax.axis_size("expert")
    capacity = 3 * tok_count * top_count // (2 * expert_count)
    swap = lambda w: lax.ppermute(w, "seq", [(0, 1), (1, 0)])
    gate, up, down = gate_weight[0], up_weight[0], down_weight[0]
    gate_far, up_far, down_far = swap(gate), swap(up), swap(down)
    named = routes.T

    position, sent = pack(named, tokens, grad_out, expert_count, capacity)
    received = exchange(sent)
    rows = expert_terms(received, down, down_far, gate, gate_far, up, up_far)
    back = exchange(rows)
    grad_tokens, grad_probs = combine(named, position, route_probs.T, back, width)
    return (grad_tokens, grad_probs.T)


def solution(mesh):
    placed = (
        P(("seq", "expert"), None),
        P(("seq", "expert"), None),
        P(("seq", "expert"), None),
        P("expert", None, "seq"),
        P("expert", None, "seq"),
        P("expert", "seq", None),
        P(("seq", "expert"), None),
    )
    return jax.shard_map(
        on_device,
        mesh=mesh,
        in_specs=placed,
        out_specs=(P(("seq", "expert"), None), P(("seq", "expert"), None)),
        check_vma=False,
    )
```

```python
import functools

import jax
import jax.numpy as jnp
from jax import lax
from jax.experimental import pallas as pl
from jax.experimental.pallas import tpu as pltpu
from jax.sharding import PartitionSpec as P

LANES = 128
CHUNK = 8
GROUP = 16
AHEAD = 8
BLOCKS = 1
PIECES = 4
MIB = 1024 * 1024
VMEM = pl.BlockSpec(memory_space=pltpu.VMEM)
SMEM = pl.BlockSpec(memory_space=pltpu.SMEM)
ANYWHERE = pl.BlockSpec(memory_space=pl.ANY)


def params(mib):
    return pltpu.CompilerParams(vmem_limit_bytes=mib * MIB)


def on_chip(x):
    return pltpu.with_memory_space_constraint(x, pltpu.VMEM)


def place_rows(rows_ref, source, blocks, stage, send):
    tok_count = rows_ref.shape[0]
    experts, capacity, parts, _ = stage.shape
    for r in range(0, tok_count, GROUP):
        blocks[r : r + GROUP] = rows_ref[r : r + GROUP, :].reshape(GROUP, parts, LANES)
    group = 4
    share = experts // PIECES

    def place(g, _):
        first = g * group
        rows = [
            [blocks[source[(first + i) * capacity + s]] for s in range(capacity)]
            for i in range(group)
        ]
        for i in range(group):
            for s in range(capacity):
                stage[first + i, s] = rows[i][s]
        return 0

    for piece in range(PIECES):
        lax.fori_loop(piece * share // group, (piece + 1) * share // group, place, 0)
        send(piece, pl.ds(piece * share, share))


def pack_kernel(
    routes_ref, tokens_hbm, grads_hbm, position_ref, out_ref,
    counts, source, tokens_ref, grads_ref, blocks, stage_in, stage_grad, sems,
):
    top, tok_count = routes_ref.shape
    capacity = stage_in.shape[1]
    load_in = pltpu.make_async_copy(tokens_hbm, tokens_ref, sems.at[0])
    load_grad = pltpu.make_async_copy(grads_hbm, grads_ref, sems.at[1])
    load_in.start()
    load_grad.start()

    def clear(e, _):
        counts[e] = 0
        for s in range(capacity):
            source[e * capacity + s] = 0
        return 0

    lax.fori_loop(0, counts.shape[0], clear, 0, unroll=8)

    def rank(t, _):
        for k in range(top):
            e = routes_ref[k, t]
            position = counts[e]
            counts[e] = position + 1
            position_ref[k, t] = position
            source[e * capacity + position] = t
        return 0

    lax.fori_loop(0, tok_count, rank, 0, unroll=8)
    sends = []

    def sender(stage, which):
        def send(piece, some):
            copy = pltpu.make_async_copy(
                stage.at[some], out_ref.at[some, which], sems.at[2 + which * PIECES + piece]
            )
            copy.start()
            sends.append(copy)

        return send

    load_in.wait()
    place_rows(tokens_ref, source, blocks, stage_in, sender(stage_in, 0))
    load_grad.wait()
    place_rows(grads_ref, source, blocks, stage_grad, sender(stage_grad, 1))
    for copy in sends:
        copy.wait()


def pack(routes, tokens, grads, expert_count, capacity):
    tok_count, width = tokens.shape
    parts = width // LANES
    stage = pltpu.VMEM((expert_count, capacity, parts, LANES), jnp.bfloat16)
    return pl.pallas_call(
        pack_kernel,
        out_shape=(
            jax.ShapeDtypeStruct(routes.shape, jnp.int32),
            jax.ShapeDtypeStruct((expert_count, 2, capacity, parts, LANES), jnp.bfloat16),
        ),
        in_specs=[SMEM, ANYWHERE, ANYWHERE],
        out_specs=(SMEM, ANYWHERE),
        scratch_shapes=[
            pltpu.SMEM((expert_count,), jnp.int32),
            pltpu.SMEM((expert_count * capacity,), jnp.int32),
            pltpu.VMEM((tok_count, width), jnp.bfloat16),
            pltpu.VMEM((tok_count, width), jnp.bfloat16),
            pltpu.VMEM((tok_count, parts, LANES), jnp.bfloat16),
            stage,
            stage,
            pltpu.SemaphoreType.DMA((2 + 2 * PIECES,)),
        ],
        compiler_params=params(62),
        name="pack",
    )(routes, tokens, grads)


def expert_kernel(
    x_hbm, d0_hbm, d1_hbm, g0_hbm, g1_hbm, u0_hbm, u1_hbm, out_ref,
    x_ref, down, gate_up, grads, wide, column, stage, in_sems, out_sems,
):
    contract = (((1,), (1,)), ((), ()))
    experts, _, capacity, parts, _ = x_hbm.shape
    rows = experts * capacity
    steps = parts // CHUNK
    depth = CHUNK * LANES
    half = d0_hbm.shape[0]
    hid = 2 * half
    dests = experts // BLOCKS
    some = dests * capacity

    def cut(step):
        return pl.ds(step * depth, depth)

    def halves(step):
        if step:
            return [cut(step)]
        return [pl.ds(0, depth // 2), pl.ds(depth // 2, depth // 2)]

    count = [0]

    def fetch(src, dst):
        count[0] += 1
        return pltpu.make_async_copy(src, dst, in_sems.at[count[0] - 1])

    def fetch_rows(which, step):
        return fetch(x_hbm.at[:, which, :, pl.ds(step * CHUNK, CHUNK)], x_ref.at[which, step])

    batches = [
        [fetch_rows(0, step)]
        + [
            fetch(src.at[rows_in], gate_up.at[rows_in, pl.ds(h * half, half)])
            for rows_in in halves(step)
            for h, src in enumerate((g0_hbm, g1_hbm, u0_hbm, u1_hbm))
        ]
        for step in range(steps)
    ] + [
        [fetch_rows(1, step)]
        + [
            fetch(src.at[:, cut(step)], down.at[pl.ds(h * half, half), cut(step)])
            for h, src in enumerate((d0_hbm, d1_hbm))
        ]
        for step in range(steps)
    ]
    for batch in batches[:AHEAD]:
        for copy in batch:
            copy.start()

    def arrive(i):
        for copy in batches[i]:
            copy.wait()
        for batch in batches[i + AHEAD : i + AHEAD + 1]:
            for copy in batch:
                copy.start()

    def taken(which, step, first, number):
        part = x_ref[which, step, first : first + number]
        return part.reshape(number * capacity, CHUNK, LANES).reshape(number * capacity, depth)

    both = None
    for step in range(steps):
        if step == 0:
            for copy in batches[0][:5]:
                copy.wait()
            got = taken(0, 0, 0, experts)
            both = jnp.dot(
                got[:, : depth // 2], gate_up[: depth // 2], preferred_element_type=jnp.float32
            )
            for copy in batches[0][5:]:
                copy.wait()
            both = both + jnp.dot(
                got[:, depth // 2 :],
                gate_up[depth // 2 : depth],
                preferred_element_type=jnp.float32,
            )
            continue
        arrive(step)
        both = both + jnp.dot(
            taken(0, step, 0, experts), gate_up[cut(step)], preferred_element_type=jnp.float32
        )
    wide[...] = both
    for step in range(steps):
        arrive(steps + step)

    for b in range(BLOCKS):
        here = slice(b * some, (b + 1) * some)
        grad_hidden = None
        for step in range(steps):
            part = lax.dot_general(
                taken(1, step, b * dests, dests),
                down[:, cut(step)],
                contract,
                preferred_element_type=jnp.float32,
            )
            grad_hidden = part if step == 0 else grad_hidden + part
        gating = wide[here, 0:hid]
        lifted = wide[here, hid : 2 * hid]
        sigmoid = jax.nn.sigmoid(gating)
        active = gating * sigmoid
        hidden = (active * lifted).astype(jnp.bfloat16)
        slope = sigmoid * (1.0 + gating * (1.0 - sigmoid))
        grads[here, 0:hid] = (grad_hidden * lifted * slope).astype(jnp.bfloat16)
        grads[here, hid : 2 * hid] = (grad_hidden * active).astype(jnp.bfloat16)
        prob = jnp.sum(hidden.astype(jnp.float32) * grad_hidden, axis=1, keepdims=True)
        column[here, :] = jnp.broadcast_to(prob, (some, LANES))

    sends = []

    def send(first, number, tile):
        places = pl.ds(first, number)
        copy = pltpu.make_async_copy(
            stage.at[places, tile], out_ref.at[places, tile], out_sems.at[len(sends)]
        )
        copy.start()
        sends.append(copy)

    for b in range(BLOCKS):
        for step in range(steps):
            part = lax.dot_general(
                grads[b * some : (b + 1) * some, :],
                gate_up[cut(step)],
                contract,
                preferred_element_type=jnp.float32,
            )
            tiles = part.astype(jnp.bfloat16).reshape(dests, capacity, CHUNK, LANES)
            for s in range(capacity):
                stage[b * dests : (b + 1) * dests, s * steps + step] = tiles[:, s]
            if b == 0 and step == 0:
                picked = [column[pl.ds(s, experts, stride=capacity), :] for s in range(capacity)]
                column[0 : experts * CHUNK, :] = jnp.zeros((experts * CHUNK, LANES), jnp.float32)
                for s in range(capacity):
                    column[pl.ds(s, experts, stride=CHUNK), :] = picked[s]
                stage[:, capacity * steps] = (
                    column[0 : experts * CHUNK, :].reshape(experts, CHUNK, LANES).astype(jnp.bfloat16)
                )
                send(0, experts, capacity * steps)
            for s in range(capacity):
                send(b * dests, dests, s * steps + step)
    for copy in sends:
        copy.wait()


def expert_terms(x, d0, d1, g0, g1, u0, u1):
    expert_count, _, capacity, parts, _ = x.shape
    rows = expert_count * capacity
    width, half = g0.shape
    hid = 2 * half
    steps = parts // CHUNK
    tiles = capacity * steps + 1
    return pl.pallas_call(
        expert_kernel,
        out_shape=jax.ShapeDtypeStruct((expert_count, tiles, CHUNK, LANES), jnp.bfloat16),
        in_specs=[ANYWHERE] * 7,
        out_specs=ANYWHERE,
        scratch_shapes=[
            pltpu.VMEM((2, steps, expert_count, capacity, CHUNK, LANES), jnp.bfloat16),
            pltpu.VMEM((hid, width), jnp.bfloat16),
            pltpu.VMEM((width, 2 * hid), jnp.bfloat16),
            pltpu.VMEM((rows, 2 * hid), jnp.bfloat16),
            pltpu.VMEM((rows, 2 * hid), jnp.float32),
            pltpu.VMEM((max(rows, expert_count * CHUNK), LANES), jnp.float32),
            pltpu.VMEM((expert_count, tiles, CHUNK, LANES), jnp.bfloat16),
            pltpu.SemaphoreType.DMA((8 * steps + 4,)),
            pltpu.SemaphoreType.DMA((BLOCKS * (tiles - 1) + 1,)),
        ],
        compiler_params=params(50),
        name="expert_terms",
    )(x, d0, d1, g0, g1, u0, u1)


def combine_kernel(routes_ref, position_ref, probs_ref, back_ref, out_ref, grad_ref, blocks):
    top, tok_count = routes_ref.shape
    parts = blocks.shape[1]
    steps = parts // CHUNK
    last = back_ref.shape[1] - 1
    group = 4
    sublane = lax.broadcasted_iota(jnp.int32, (CHUNK, LANES), 0)
    lane = lax.broadcasted_iota(jnp.int32, (CHUNK, LANES), 1)

    def gather(g, picked):
        picked = list(picked)
        rows = []
        for i in range(group):
            t = g * group + i
            total = None
            for k in range(top):
                e, position = routes_ref[k, t], position_ref[k, t]
                row = back_ref[e, pl.ds(position * steps, steps)].reshape(parts, LANES)
                term = probs_ref[k, t] * row.astype(jnp.float32)
                total = term if k == 0 else total + term
                tile = back_ref[e, last].astype(jnp.float32)
                here = (sublane == position) & (lane == t)
                picked[k] = jnp.where(here, tile, picked[k])
            rows.append(total.astype(jnp.bfloat16))
        for i in range(group):
            blocks[g * group + i] = rows[i]
        return tuple(picked)

    start = tuple(jnp.zeros((CHUNK, LANES), jnp.float32) for _ in range(top))
    picked = lax.fori_loop(0, tok_count // group, gather, start)
    grad_ref[...] = jnp.concatenate(
        [jnp.sum(p, axis=0, keepdims=True) for p in picked], axis=0
    ).astype(jnp.bfloat16)
    for r in range(0, tok_count, GROUP):
        out_ref[r : r + GROUP, :] = blocks[r : r + GROUP].reshape(GROUP, parts * LANES)


def combine(routes, position, probs, back, width):
    top, tok_count = routes.shape
    return pl.pallas_call(
        combine_kernel,
        out_shape=(
            jax.ShapeDtypeStruct((tok_count, width), jnp.bfloat16),
            jax.ShapeDtypeStruct((top, tok_count), jnp.bfloat16),
        ),
        in_specs=[SMEM, SMEM, SMEM, VMEM],
        out_specs=(VMEM, VMEM),
        scratch_shapes=[pltpu.VMEM((tok_count, width // LANES, LANES), jnp.bfloat16)],
        compiler_params=params(56),
        name="combine",
    )(routes, position, probs, on_chip(back))


def exchange(blocks):
    sent = blocks.reshape(blocks.shape[0], -1, blocks.shape[-1])
    got = lax.all_to_all(sent, "expert", split_axis=0, concat_axis=0, tiled=True)
    return got.reshape(blocks.shape)


def on_device(tokens, routes, route_probs, gate_weight, up_weight, down_weight, grad_out):
    tok_count, width = tokens.shape
    top_count = routes.shape[1]
    expert_count = lax.axis_size("expert")
    capacity = 3 * tok_count * top_count // (2 * expert_count)
    swap = lambda w: lax.ppermute(w, "seq", [(0, 1), (1, 0)])
    gate, up, down = gate_weight[0], up_weight[0], down_weight[0]
    gate_far, up_far, down_far = swap(gate), swap(up), swap(down)
    named = routes.T

    position, sent = pack(named, tokens, grad_out, expert_count, capacity)
    received = exchange(sent)
    rows = expert_terms(received, down, down_far, gate, gate_far, up, up_far)
    back = exchange(rows)
    grad_tokens, grad_probs = combine(named, position, route_probs.T, back, width)
    return (grad_tokens, grad_probs.T)


def solution(mesh):
    placed = (
        P(("seq", "expert"), None),
        P(("seq", "expert"), None),
        P(("seq", "expert"), None),
        P("expert", None, "seq"),
        P("expert", None, "seq"),
        P("expert", "seq", None),
        P(("seq", "expert"), None),
    )
    return jax.shard_map(
        on_device,
        mesh=mesh,
        in_specs=placed,
        out_specs=(P(("seq", "expert"), None), P(("seq", "expert"), None)),
        check_vma=False,
    )
```
